512 devices in a mesh: group: 16 (over y, core), leaf: 32 (over z, x).
Axes of the slice: x: 4, y: 8, z: 8, core: 2. Of those that a mesh axis runs over, the one named last changes fastest.
Arguments:
- left_vectors: float32 [256, 128], replicated, may hold values from -6 to 6
- panel_vectors: bfloat16 [2, 256, 128], replicated, may hold values from -0.375 to 0.375
- panel_factors: float32 [2, 128, 128], replicated, may hold values from -0.5 to 0.5
- node_y: bfloat16 [16, 32, 9, 256, 256], P('group', 'leaf')
- node_t: float32 [16, 32, 9, 128, 256], P('group', 'leaf'), as said below
- leaf_v: bfloat16 [262144, 256], P(('group', 'leaf')), may hold values from -0.375 to 0.375
- leaf_t: float32 [16, 32, 256, 256], P('group', 'leaf'), may hold values from -0.1875 to 0.1875
- leaf_map: int32 [16, 32], P('group', 'leaf'), may hold values from 0 to 31, as said below
Outputs:
- eofs: bfloat16 [262144, 128], P(('group', 'leaf'))
The draws below stay inside these ranges and needn't reach their ends.
Inputs may be any that keep to these rules, and one draw needn't show every extreme that they name: leaf_map[g, s] is the leaf index of the device of group g that holds leaf slot s; slots 2m and 2m + 1 name devices 2m and 2m + 1 in either order. Every device that a node of level l covers holds the same node_y[., ., l]; every device in the first half of the node's devices holds the same node_t[., ., l], and so does every device in the second half.
All inputs are finite; a program needn't handle non-finite values.
Results may differ from the reference program's by a relative error of at most 0.0045.
Values sent between devices are 32-bit elements; how exact they have to be, the bound alone decides.
No kernel may reach another device: no remote copies, remote signals or barrier semaphores. Data moves between devices by JAX's collectives and lax.ppermute only.
A program may use at most 64 MiB of HBM per device.

```python
import jax
import jax.numpy as jnp
from jax import lax

NSNAP = 256
KVEC = 128
PANEL = 128
ROWS_DEV = 512
PANELS = 2
GROUPS = 16
SLOTS = 32
LEVELS = 9
ROWS = 262144


def node_codes():
    device_total = GROUPS * SLOTS
    device = jnp.arange(device_total, dtype=jnp.int32)[:, None]
    tree_level = jnp.arange(LEVELS, dtype=jnp.int32)[None, :]
    block_size = jnp.right_shift(jnp.int32(device_total), tree_level)
    node_number = device // block_size
    lower_side = (device % block_size >= block_size // 2).astype(jnp.int32)
    codes = tree_level * device_total + node_number
    return (codes.reshape(-1), lower_side.reshape(-1))


def draw_node_t(key, part):
    codes, lower_side = node_codes()

    def draw_one(code, side_bit):
        sub_key = jax.random.fold_in(jax.random.fold_in(key, 11), code * 2 + side_bit)
        return jax.random.normal(sub_key, (NSNAP // 2, NSNAP), jnp.float32) * (4.0 * NSNAP) ** (-0.5)
    drawn = jax.vmap(draw_one)(codes, lower_side)
    return drawn.reshape(GROUPS, SLOTS, LEVELS, NSNAP // 2, NSNAP)


def draw_node_y(key, part):
    codes, lower_side = node_codes()

    def draw_one(code):
        sub_key = jax.random.fold_in(jax.random.fold_in(key, 23), code)
        return jax.random.normal(sub_key, (NSNAP, NSNAP), jnp.float32) * (NSNAP / 4.0) ** (-0.5)
    drawn = jax.vmap(draw_one)(codes)
    return drawn.reshape(GROUPS, SLOTS, LEVELS, NSNAP, NSNAP).astype(jnp.bfloat16)


def draw_leaf_map(key, part):
    flipped = jax.random.randint(key, (GROUPS, SLOTS // 2), 0, 2)
    widened = jnp.repeat(flipped, 2, axis=1)
    position = jnp.arange(SLOTS, dtype=jnp.int32)[None, :]
    return (position + widened * (1 - 2 * (position % 2))).astype(jnp.int32)


def steps_of(key, extent, cuts, low, top_value):
    factor_of, own = 1.0, jax.random.fold_in(key, 6)
    for dim, shards_of in cuts:
        steps = jnp.exp(jax.random.uniform(jax.random.fold_in(own, dim), (shards_of,), jnp.float32, low / len(cuts), top_value / len(cuts)))
        factor_of = factor_of * jnp.repeat(steps, extent[dim] // shards_of).reshape([-1 if axis == dim else 1 for axis in range(len(extent))])
    return factor_of


def normal_values(stream_key, extent, spread, limit, cuts=(), held_as=jnp.bfloat16):
    entries = jax.random.normal(stream_key, extent, jnp.float32) * spread
    if len(cuts) > 0:
        entries = steps_of(stream_key, extent, cuts, -0.22, 0.18) * entries
    return jnp.clip(entries, min=-limit, max=limit).astype(held_as)


def setup_inputs(seed: int = 0) -> dict:
    arg_keys = jax.random.split(jax.random.key(seed), 9)
    left_vectors = normal_values(arg_keys[0], (NSNAP, KVEC), 1.0, 6.0, (), jnp.float32)
    panel_vectors = normal_values(arg_keys[1], (PANELS, NSNAP, PANEL), NSNAP ** -0.5, 0.375)
    panel_factors = normal_values(arg_keys[2], (PANELS, PANEL, PANEL), PANEL ** -0.5, 0.5, (), jnp.float32)
    node_y = draw_node_y(jax.random.fold_in(arg_keys[8], 71), 0)
    node_t = draw_node_t(jax.random.fold_in(arg_keys[8], 71), 0)
    leaf_v = normal_values(arg_keys[5], (ROWS, NSNAP), NSNAP ** -0.5, 0.375, ((0, 512),))
    leaf_t = normal_values(arg_keys[6], (GROUPS, SLOTS, NSNAP, NSNAP), (4 * NSNAP) ** -0.5, 0.1875, ((0, 16), (1, 32)), jnp.float32)
    leaf_map = draw_leaf_map(jax.random.fold_in(arg_keys[8], 71), 0)
    return {"left_vectors": left_vectors, "panel_vectors": panel_vectors, "panel_factors": panel_factors, "node_y": node_y, "node_t": node_t, "leaf_v": leaf_v, "leaf_t": leaf_t, "leaf_map": leaf_map}


highest = lax.Precision.HIGHEST


def back_panels(vectors, panel_vectors, panel_factors):
    result = vectors
    panel_count = panel_vectors.shape[0]
    for panel_index in range(panel_count - 1, -1, -1):
        reflect = panel_vectors[panel_index].astype(jnp.float32)
        projected = jnp.dot(reflect.T, result, precision=highest)
        scaled = jnp.dot(panel_factors[panel_index], projected, precision=highest)
        result = result - jnp.dot(reflect, scaled, precision=highest)
    return result


def leaf_apply(operands):
    leaf_block, factor, incoming, rounded = operands
    projected = jnp.dot(leaf_block[:NSNAP].T, rounded, preferred_element_type=jnp.float32)
    solved = jnp.dot(factor, projected, precision=highest).astype(jnp.bfloat16)
    applied = jnp.dot(leaf_block, solved, preferred_element_type=jnp.float32)
    extended = jnp.concatenate([incoming, jnp.zeros((ROWS_DEV - NSNAP, KVEC), jnp.float32)], axis=0)
    return (extended - applied).astype(jnp.bfloat16)


def reference(left_vectors, panel_vectors, panel_factors, node_y, node_t, leaf_v, leaf_t, leaf_map):
    device_total = GROUPS * SLOTS
    root_vectors = back_panels(left_vectors, panel_vectors, panel_factors)
    factor_rows = node_t.reshape(device_total, LEVELS, NSNAP // 2, NSNAP)
    reflect_all = node_y.reshape(device_total, LEVELS, NSNAP, NSNAP)
    current = root_vectors[None]
    for tree_level in range(LEVELS):
        block_size = device_total // (2 ** tree_level)
        top_owners = jnp.arange(0, device_total, block_size, dtype=jnp.int32)
        bottom_owners = top_owners + block_size // 2
        factor_t = jnp.concatenate([factor_rows[top_owners, tree_level], factor_rows[bottom_owners, tree_level]], axis=1)
        factor_y = reflect_all[bottom_owners, tree_level].astype(jnp.float32)
        weighted = jnp.einsum('nij,njk->nik', factor_t, current, precision=highest)
        upper_half = current - weighted
        lower_half = -jnp.einsum('nij,njk->nik', factor_y, weighted, precision=highest)
        current = jnp.stack([upper_half, lower_half], axis=1).reshape(-1, NSNAP, KVEC)
    slot_vectors = current.reshape(GROUPS, SLOTS, NSNAP, KVEC)
    slot_numbers = jnp.broadcast_to(jnp.arange(SLOTS, dtype=jnp.int32)[None, :], (GROUPS, SLOTS))
    group_numbers = jnp.arange(GROUPS, dtype=jnp.int32)[:, None]
    inverse = jnp.zeros((GROUPS, SLOTS), jnp.int32).at[group_numbers, leaf_map].set(slot_numbers)
    device_x = slot_vectors[group_numbers, inverse].reshape(device_total, NSNAP, KVEC)
    rounded = device_x.astype(jnp.bfloat16)
    blocks = leaf_v.reshape(device_total, ROWS_DEV, NSNAP)
    factors = leaf_t.reshape(device_total, NSNAP, NSNAP)
    results = lax.map(leaf_apply, (blocks, factors, device_x, rounded))
    return results.reshape(ROWS, KVEC)
```

```python
import jax
import jax.numpy as jnp
from jax import lax
from jax.experimental import pallas as pl
from jax.experimental.pallas import tpu as pltpu
from jax.sharding import PartitionSpec as P


ANY = pl.BlockSpec(memory_space=pl.ANY)
VMEM = pl.BlockSpec(memory_space=pltpu.VMEM)
SMEM = pl.BlockSpec(memory_space=pltpu.SMEM)
f32 = jnp.float32
bf16 = jnp.bfloat16


def halves(value):
    high = value.astype(bf16)
    low = (value - high.astype(f32)).astype(bf16)
    return high, low


def mul(left, right):
    return jnp.dot(left, right, preferred_element_type=f32)


def exact_times(exact, value):
    columns = value.shape[1]
    both = mul(exact, jnp.concatenate(halves(value), axis=1))
    return both[:, :columns] + both[:, columns:]


def split_times(high, low, value):
    columns = value.shape[1]
    value_high, value_low = halves(value)
    both = mul(high, jnp.concatenate([value_high, value_low], axis=1))
    return both[:, :columns] + both[:, columns:] + mul(low, value_high)


def ring_partner(place):
    return (place + 1) % 8 if place % 2 else (place - 1) % 8


def ring_outer(place):
    return (place & 1) == ((place >> 1) & 1)


def places():
    group = lax.axis_index("group")
    leaf = lax.axis_index("leaf")
    return group >> 1, group & 1, leaf >> 2, leaf & 3


def pieces_kernel(node_t, own, y_send, z_send, seven, eight, three, sems):
    y, _, z, _ = places()
    y_level = jnp.where(ring_outer(y), 0, 1)
    z_level = jnp.where(ring_outer(z), 4, 5)
    copies = [
        pltpu.make_async_copy(node_t.at[0, 0, level], out, sems.at[i])
        for i, (level, out) in enumerate(
            [(y_level, y_send), (z_level, z_send), (7, seven), (8, eight), (3, three)]
        )
    ]
    copies.append(pltpu.make_async_copy(node_t.at[0, 0], own, sems.at[5]))
    for copy in copies:
        copy.start()
    for copy in copies:
        copy.wait()


def in_vmem(array):
    return pltpu.with_memory_space_constraint(array, pltpu.VMEM)


def pieces(node_t):
    shape = pltpu.VMEM((128, 256), f32)
    return pl.pallas_call(
        pieces_kernel,
        out_shape=(pltpu.VMEM((9, 128, 256), f32),) + (shape,) * 5,
        in_specs=[ANY],
        out_specs=(VMEM,) * 6,
        scratch_shapes=[pltpu.SemaphoreType.DMA((6,))],
        name="pieces",
    )(node_t)


def join(own, received, level, name):
    def kernel(own, received, out):
        out[0] = own[level]
        out[1] = received[...]

    return pl.pallas_call(
        kernel,
        out_shape=pltpu.VMEM((2, 128, 256), f32),
        in_specs=[VMEM, VMEM],
        out_specs=VMEM,
        name=name,
    )(in_vmem(own), in_vmem(received))


def place_rows(high_ref, low_ref, slot, bit, value):
    rows = pl.ds(pl.multiple_of(bit * 128, 128), 128)
    high, low = halves(value)
    high_ref[slot, rows] = high
    low_ref[slot, rows] = low


def step(x_ref, high, low, reflect, lower):
    weighted = split_times(high, low, x_ref[...])

    @pl.when(lower == 1)
    def _():
        x_ref[...] = -exact_times(reflect[...], weighted)

    @pl.when(lower == 0)
    def _():
        x_ref[...] = x_ref[...] - weighted


def group_kernel(
    left, vectors, factors, node_y, own, y_got, y_pair, three, x_out,
    reflect, high_ref, low_ref, sems,
):
    y, core, _, _ = places()
    outer = ring_outer(y)
    row = jnp.where(outer, 0, 1)
    bits = [(y >> 2) & 1, (y >> 1) & 1, y & 1, core]
    loads = [
        pltpu.make_async_copy(node_y.at[0, 0, i], reflect.at[i], sems.at[i]) for i in range(4)
    ]
    for load in loads:
        load.start()

    x = left[...]
    for panel in (1, 0):
        vector = vectors[panel]
        columns = x.shape[1]
        both = lax.dot_general(
            vector,
            jnp.concatenate(halves(x), axis=1),
            (((0,), (0,)), ((), ())),
            preferred_element_type=f32,
        )
        projected = both[:, :columns] + both[:, columns:]
        scaled = split_times(*halves(factors[panel]), projected)
        x = x - exact_times(vector, scaled)
    x_out[...] = x

    ring_bit = jnp.where(outer, bits[0], bits[1])
    pair_bit = jnp.where(outer, bits[1], bits[0])
    for i in range(4):
        place_rows(high_ref, low_ref, i, bits[i], own[i])
    place_rows(high_ref, low_ref, row, 1 - ring_bit, y_got[...])
    place_rows(high_ref, low_ref, 1 - row, 1 - pair_bit, y_pair[1])
    place_rows(high_ref, low_ref, 2, 1 - bits[2], y_pair[0])
    place_rows(high_ref, low_ref, 3, 1 - bits[3], three[...])
    for i in range(4):
        loads[i].wait()
        step(x_out, high_ref[i], low_ref[i], reflect.at[i], bits[i])


def leaf_kernel(
    x_in, node_y, own, z_got, z_pair, seven, eight, leaf_v, leaf_t, leaf_map, out,
    x_ref, reflect, high_ref, low_ref, v_ref, t_ref, sems,
):
    _, _, z, x_place = places()
    outer = ring_outer(z)
    row = jnp.where(outer, 0, 1)
    bits = [(z >> 2) & 1, (z >> 1) & 1, z & 1, (x_place >> 1) & 1, x_place & 1]
    loads = [
        pltpu.make_async_copy(node_y.at[0, 0, 4 + i], reflect.at[i], sems.at[i]) for i in range(5)
    ]
    load_v = pltpu.make_async_copy(leaf_v, v_ref, sems.at[5])
    load_t = pltpu.make_async_copy(leaf_t.at[0, 0], t_ref, sems.at[6])
    for load in loads + [load_v, load_t]:
        load.start()
    x_ref[...] = x_in[...]
    flipped = leaf_map[0, 0] != lax.axis_index("leaf")
    last = jnp.where(flipped, 1 - bits[4], bits[4])
    lows = bits[:4] + [last]
    ring_bit = jnp.where(outer, bits[0], bits[1])
    pair_bit = jnp.where(outer, bits[1], bits[0])
    for i in range(5):
        place_rows(high_ref, low_ref, i, bits[i], own[4 + i])
    place_rows(high_ref, low_ref, row, 1 - ring_bit, z_got[...])
    place_rows(high_ref, low_ref, 1 - row, 1 - pair_bit, z_pair[1])
    place_rows(high_ref, low_ref, 2, 1 - bits[2], z_pair[0])
    place_rows(high_ref, low_ref, 3, 1 - bits[3], seven[...])
    place_rows(high_ref, low_ref, 4, 1 - bits[4], eight[...])
    for i in range(5):
        loads[i].wait()
        step(x_ref, high_ref[i], low_ref[i], reflect.at[i], lows[i])
    load_v.wait()
    load_t.wait()
    x = x_ref[...]
    projected = lax.dot_general(
        v_ref[:256], x.astype(bf16), (((0,), (0,)), ((), ())), preferred_element_type=f32
    )
    solved = split_times(*halves(t_ref[...]), projected).astype(bf16)
    out[:256] = (x - mul(v_ref[:256], solved)).astype(bf16)
    out[256:] = (-mul(v_ref[256:], solved)).astype(bf16)


def exchange(block, axis, partner):
    count = lax.axis_size(axis)
    return lax.ppermute(block, axis, [(place, partner(place)) for place in range(count)])


def on_device(left_vectors, panel_vectors, panel_factors, node_y, node_t, leaf_v, leaf_t, leaf_map):
    own, y_send, z_send, seven, eight, three = pieces(node_t)
    y_got = exchange(y_send, "group", lambda g: ring_partner(g >> 1) * 2 + (g & 1))
    z_got = exchange(z_send, "leaf", lambda j: ring_partner(j >> 2) * 4 + (j & 3))
    seven_got = exchange(seven, "leaf", lambda j: j ^ 3)
    y_pair = exchange(join(own, y_got, 2, "join_y"), "group", lambda g: g ^ 2)
    z_pair = exchange(join(own, z_got, 6, "join_z"), "leaf", lambda j: j ^ 4)
    eight_got = exchange(eight, "leaf", lambda j: j ^ 1)
    three_got = exchange(three, "group", lambda g: g ^ 1)
    x = pl.pallas_call(
        group_kernel,
        out_shape=pltpu.VMEM((256, 128), f32),
        in_specs=[VMEM, VMEM, VMEM, ANY] + [VMEM] * 4,
        out_specs=VMEM,
        scratch_shapes=[
            pltpu.VMEM((4, 256, 256), bf16),
            pltpu.VMEM((4, 256, 256), bf16),
            pltpu.VMEM((4, 256, 256), bf16),
            pltpu.SemaphoreType.DMA((4,)),
        ],
        name="group_levels",
    )(
        left_vectors, panel_vectors, panel_factors, node_y,
        in_vmem(own), in_vmem(y_got), in_vmem(y_pair), in_vmem(three_got),
    )
    return pl.pallas_call(
        leaf_kernel,
        out_shape=jax.ShapeDtypeStruct((512, 128), bf16),
        in_specs=[VMEM, ANY] + [VMEM] * 5 + [ANY, ANY, SMEM],
        out_specs=VMEM,
        scratch_shapes=[
            pltpu.VMEM((256, 128), f32),
            pltpu.VMEM((5, 256, 256), bf16),
            pltpu.VMEM((5, 256, 256), bf16),
            pltpu.VMEM((5, 256, 256), bf16),
            pltpu.VMEM((512, 256), bf16),
            pltpu.VMEM((256, 256), f32),
            pltpu.SemaphoreType.DMA((7,)),
        ],
        name="leaf_levels",
    )(
        in_vmem(x), node_y, in_vmem(own), in_vmem(z_got), in_vmem(z_pair),
        in_vmem(seven_got), in_vmem(eight_got), leaf_v, leaf_t, leaf_map,
    )


def solution(mesh):
    return jax.shard_map(
        on_device,
        mesh=mesh,
        in_specs=(
            P(),
            P(),
            P(),
            P("group", "leaf", None, None, None),
            P("group", "leaf", None, None, None),
            P(("group", "leaf"), None),
            P("group", "leaf", None, None),
            P("group", "leaf"),
        ),
        out_specs=P(("group", "leaf"), None),
        check_vma=False,
    )
```

```python
import jax
import jax.numpy as jnp
from jax import lax
from jax.experimental import pallas as pl
from jax.experimental.pallas import tpu as pltpu
from jax.sharding import PartitionSpec as P


ANY = pl.BlockSpec(memory_space=pl.ANY)
VMEM = pl.BlockSpec(memory_space=pltpu.VMEM)
SMEM = pl.BlockSpec(memory_space=pltpu.SMEM)
SMALL = pltpu.CompilerParams(vmem_limit_bytes=8 << 20)
f32 = jnp.float32
bf16 = jnp.bfloat16


def halves(value):
    high = value.astype(bf16)
    low = (value - high.astype(f32)).astype(bf16)
    return high, low


def mul(left, right):
    return jnp.dot(left, right, preferred_element_type=f32)


def exact_times(exact, value):
    columns = value.shape[1]
    both = mul(exact, jnp.concatenate(halves(value), axis=1))
    return both[:, :columns] + both[:, columns:]


def split_times(high, low, value):
    columns = value.shape[1]
    value_high, value_low = halves(value)
    both = mul(high, jnp.concatenate([value_high, value_low], axis=1))
    return both[:, :columns] + both[:, columns:] + mul(low, value_high)


def ring_partner(place):
    return (place + 1) % 8 if place % 2 else (place - 1) % 8


def ring_outer(place):
    return (place & 1) == ((place >> 1) & 1)


def places():
    group = lax.axis_index("group")
    leaf = lax.axis_index("leaf")
    return group >> 1, group & 1, leaf >> 2, leaf & 3


def is_ahead(z):
    return z == 0


def ahead():
    return is_ahead(lax.axis_index("leaf") >> 2)


def pieces_kernel(node_t, y_send, z_send, seven, eight, three, sems):
    y, _, z, _ = places()
    y_level = jnp.where(ring_outer(y), 0, 1)
    z_level = jnp.where(ring_outer(z), 4, 5)
    copies = [
        pltpu.make_async_copy(node_t.at[0, 0, level], out, sems.at[i])
        for i, (level, out) in enumerate(
            [(y_level, y_send), (z_level, z_send), (7, seven), (8, eight), (3, three)]
        )
    ]
    for copy in copies:
        copy.start()
    for copy in copies:
        copy.wait()


def in_vmem(array):
    return pltpu.with_memory_space_constraint(array, pltpu.VMEM)


def pieces(node_t):
    shape = pltpu.VMEM((128, 256), f32)
    return pl.pallas_call(
        pieces_kernel,
        out_shape=(shape,) * 5,
        in_specs=[ANY],
        out_specs=(VMEM,) * 5,
        scratch_shapes=[pltpu.SemaphoreType.DMA((5,))],
        name="pieces",
        compiler_params=SMALL,
    )(node_t)


def join(own, received, level):
    def kernel(own, *refs):
        out = refs[-1]
        out[0] = own[0, 0, level]
        if len(refs) == 2:
            out[1] = refs[0][...]
        else:
            out[1] = jnp.where(ahead(), refs[0][...], refs[1][...])

    return pl.pallas_call(
        kernel,
        out_shape=pltpu.VMEM((2, 128, 256), f32),
        in_specs=[VMEM] * (1 + len(received)),
        out_specs=VMEM,
        compiler_params=SMALL,
    )(own, *[in_vmem(array) for array in received])


def place_rows(high_ref, low_ref, slot, bit, value):
    rows = pl.ds(pl.multiple_of(bit * 128, 128), 128)
    high, low = halves(value)
    high_ref[slot, rows] = high
    low_ref[slot, rows] = low


def tree_step(x_ref, high, low, reflect, lower):
    weighted = split_times(high, low, x_ref[...])

    @pl.when(lower == 1)
    def _():
        x_ref[...] = -exact_times(reflect[...], weighted)

    @pl.when(lower == 0)
    def _():
        x_ref[...] = x_ref[...] - weighted


def group_kernel(
    left, vectors, factors, node_y, own, y_got, y_late, y_pair, three, x_out,
    high_ref, low_ref,
):
    y, core, _, _ = places()
    outer = ring_outer(y)
    row = jnp.where(outer, 0, 1)
    bits = [(y >> 2) & 1, (y >> 1) & 1, y & 1, core]

    x = left[...]
    for panel in (1, 0):
        vector = vectors[panel]
        columns = x.shape[1]
        both = lax.dot_general(
            vector,
            jnp.concatenate(halves(x), axis=1),
            (((0,), (0,)), ((), ())),
            preferred_element_type=f32,
        )
        projected = both[:, :columns] + both[:, columns:]
        scaled = split_times(*halves(factors[panel]), projected)
        x = x - exact_times(vector, scaled)
    x_out[...] = x

    ring_bit = jnp.where(outer, bits[0], bits[1])
    pair_bit = jnp.where(outer, bits[1], bits[0])
    for i in range(4):
        place_rows(high_ref, low_ref, i, bits[i], own[0, 0, i])
    place_rows(high_ref, low_ref, row, 1 - ring_bit, jnp.where(ahead(), y_got[...], y_late[...]))
    place_rows(high_ref, low_ref, 1 - row, 1 - pair_bit, y_pair[1])
    place_rows(high_ref, low_ref, 2, 1 - bits[2], y_pair[0])
    place_rows(high_ref, low_ref, 3, 1 - bits[3], three[...])
    for i in range(4):
        tree_step(x_out, high_ref[i], low_ref[i], node_y.at[0, 0, i], bits[i])


def leaf_kernel(
    x_in, node_y, own, z_got, z_pair, seven, eight, eight_late, leaf_v, leaf_t, leaf_map, out,
    x_ref, high_ref, low_ref,
):
    _, _, z, x_place = places()
    outer = ring_outer(z)
    row = jnp.where(outer, 0, 1)
    bits = [(z >> 2) & 1, (z >> 1) & 1, z & 1, (x_place >> 1) & 1, x_place & 1]
    x_ref[...] = x_in[...]
    flipped = leaf_map[0, 0] != lax.axis_index("leaf")
    last = jnp.where(flipped, 1 - bits[4], bits[4])
    lows = bits[:4] + [last]
    ring_bit = jnp.where(outer, bits[0], bits[1])
    pair_bit = jnp.where(outer, bits[1], bits[0])
    for i in range(5):
        place_rows(high_ref, low_ref, i, bits[i], own[0, 0, 4 + i])
    place_rows(high_ref, low_ref, row, 1 - ring_bit, z_got[...])
    place_rows(high_ref, low_ref, 1 - row, 1 - pair_bit, z_pair[1])
    place_rows(high_ref, low_ref, 2, 1 - bits[2], z_pair[0])
    place_rows(high_ref, low_ref, 3, 1 - bits[3], seven[...])
    place_rows(high_ref, low_ref, 4, 1 - bits[4], jnp.where(ahead(), eight[...], eight_late[...]))
    for i in range(5):
        tree_step(x_ref, high_ref[i], low_ref[i], node_y.at[0, 0, 4 + i], lows[i])
    x = x_ref[...]
    projected = lax.dot_general(
        leaf_v[:256], x.astype(bf16), (((0,), (0,)), ((), ())), preferred_element_type=f32
    )
    solved = split_times(*halves(leaf_t[0, 0]), projected).astype(bf16)
    out[:256] = (x - mul(leaf_v[:256], solved)).astype(bf16)
    out[256:] = (-mul(leaf_v[256:], solved)).astype(bf16)


def exchange(block, partner, planes=None):
    pairs = []
    for g in range(16):
        for j in range(32):
            place = (g >> 1, g & 1, j >> 2, j & 3)
            if planes is None or planes(place[2]):
                y, core, z, x = partner(*place)
                pairs.append((g * 32 + j, (y * 2 + core) * 32 + z * 4 + x))
    return lax.ppermute(block, ("group", "leaf"), pairs)


def is_behind(z):
    return not is_ahead(z)


def body(left_vectors, panel_vectors, panel_factors, node_y, node_t, leaf_v, leaf_t, leaf_map):
    def y_ring(y, core, z, x):
        return ring_partner(y), core, z, x

    def z_ring(y, core, z, x):
        return y, core, ring_partner(z), x

    def y_next(y, core, z, x):
        return y ^ 1, core, z, x

    def z_next(y, core, z, x):
        return y, core, z ^ 1, x

    def x_far(y, core, z, x):
        return y, core, z, x ^ 3

    def x_next(y, core, z, x):
        return y, core, z, x ^ 1

    def other_core(y, core, z, x):
        return y, 1 - core, z, x

    y_send, z_send, seven, eight, three = pieces(pltpu.with_memory_space_constraint(node_t, pltpu.HBM))
    own, node_y, leaf_v, leaf_t = [in_vmem(array) for array in (node_t, node_y, leaf_v, leaf_t)]
    y_got = [exchange(y_send, y_ring, is_ahead)]
    eight_got = [exchange(eight, x_next, is_ahead)]
    z_got = exchange(z_send, z_ring)
    y_got.append(exchange(y_send, y_ring, is_behind))
    eight_got.append(exchange(eight, x_next, is_behind))
    three_got = exchange(three, other_core)
    y_pair = exchange(join(own, y_got, 2), y_next)
    z_pair = exchange(join(own, [z_got], 6), z_next)
    seven_got = exchange(seven, x_far)
    x = pl.pallas_call(
        group_kernel,
        out_shape=pltpu.VMEM((256, 128), f32),
        in_specs=[VMEM] * 9,
        out_specs=VMEM,
        scratch_shapes=[pltpu.VMEM((4, 256, 256), bf16)] * 2,
        name="group_kernel",
        compiler_params=SMALL,
    )(
        in_vmem(left_vectors), in_vmem(panel_vectors), in_vmem(panel_factors), node_y, own,
        *[in_vmem(array) for array in (*y_got, y_pair, three_got)],
    )
    return pl.pallas_call(
        leaf_kernel,
        out_shape=jax.ShapeDtypeStruct((512, 128), bf16),
        in_specs=[VMEM] * 10 + [SMEM],
        out_specs=VMEM,
        scratch_shapes=[pltpu.VMEM((256, 128), f32)] + [pltpu.VMEM((5, 256, 256), bf16)] * 2,
        name="leaf_kernel",
        compiler_params=SMALL,
    )(
        in_vmem(x), node_y, own, *[in_vmem(array) for array in (z_got, z_pair, seven_got, *eight_got)],
        leaf_v, leaf_t, leaf_map,
    )


def solution(mesh):
    return jax.shard_map(
        body,
        mesh=mesh,
        in_specs=(
            P(),
            P(),
            P(),
            P("group", "leaf", None, None, None),
            P("group", "leaf", None, None, None),
            P(("group", "leaf"), None),
            P("group", "leaf", None, None),
            P("group", "leaf"),
        ),
        out_specs=P(("group", "leaf"), None),
        check_vma=False,
    )
```

```python
import jax
import jax.numpy as jnp
from jax import lax
from jax.experimental import pallas as pl
from jax.experimental.pallas import tpu as pltpu
from jax.sharding import PartitionSpec as P


ANY = pl.BlockSpec(memory_space=pl.ANY)
VMEM = pl.BlockSpec(memory_space=pltpu.VMEM)
SMALL = pltpu.CompilerParams(vmem_limit_bytes=8 << 20)
f32 = jnp.float32
bf16 = jnp.bfloat16


def halves(value):
    high = value.astype(bf16)
    low = (value - high.astype(f32)).astype(bf16)
    return high, low


def mul(left, right):
    return jnp.dot(left, right, preferred_element_type=f32)


def exact_times(exact, value):
    columns = value.shape[1]
    both = mul(exact, jnp.concatenate(halves(value), axis=1))
    return both[:, :columns] + both[:, columns:]


def split_times(high, low, value):
    columns = value.shape[1]
    value_high, value_low = halves(value)
    both = mul(high, jnp.concatenate([value_high, value_low], axis=1))
    return both[:, :columns] + both[:, columns:] + mul(low, value_high)


def ring_partner(place):
    return (place + 1) % 8 if place % 2 else (place - 1) % 8


def ring_outer(place):
    return (place & 1) == ((place >> 1) & 1)


def places():
    group = lax.axis_index("group")
    leaf = lax.axis_index("leaf")
    return group >> 1, group & 1, leaf >> 2, leaf & 3


def y_ahead(y, z):
    return (z == 0) | (z == 3)


def eight_ahead(y, z):
    return z == 0


def pieces_kernel(node_t, y_send, z_send, seven, eight, three, sems):
    y, _, z, _ = places()
    y_level = jnp.where(ring_outer(y), 0, 1)
    z_level = jnp.where(ring_outer(z), 4, 5)
    copies = [
        pltpu.make_async_copy(node_t.at[0, 0, level], out, sems.at[i])
        for i, (level, out) in enumerate(
            [(y_level, y_send), (z_level, z_send), (7, seven), (8, eight), (3, three)]
        )
    ]
    for copy in copies:
        copy.start()
    for copy in copies:
        copy.wait()


def in_vmem(array):
    return pltpu.with_memory_space_constraint(array, pltpu.VMEM)


def pieces(node_t):
    shape = pltpu.VMEM((128, 256), f32)
    return pl.pallas_call(
        pieces_kernel,
        out_shape=(shape,) * 5,
        in_specs=[ANY],
        out_specs=(VMEM,) * 5,
        scratch_shapes=[pltpu.SemaphoreType.DMA((5,))],
        name="pieces",
        compiler_params=SMALL,
    )(node_t)


def join(own, received, level):
    def kernel(own, *refs):
        out = refs[-1]
        out[0] = own[0, 0, level]
        if len(refs) == 2:
            out[1] = refs[0][...]
        else:
            y, _, z, _ = places()
            out[1] = jnp.where(y_ahead(y, z), refs[0][...], refs[1][...])

    return pl.pallas_call(
        kernel,
        out_shape=pltpu.VMEM((2, 128, 256), f32),
        in_specs=[VMEM] * (1 + len(received)),
        out_specs=VMEM,
        compiler_params=SMALL,
    )(*[in_vmem(array) for array in (own, *received)])


def place_rows(high_ref, low_ref, slot, bit, value):
    rows = pl.ds(pl.multiple_of(bit * 128, 128), 128)
    high, low = halves(value)
    high_ref[slot, rows] = high
    low_ref[slot, rows] = low


def tree_step(x_ref, high, low, reflect, lower):
    weighted = split_times(high, low, x_ref[...])

    @pl.when(lower == 1)
    def _():
        x_ref[...] = -exact_times(reflect[...], weighted)

    @pl.when(lower == 0)
    def _():
        x_ref[...] = x_ref[...] - weighted


def root_kernel(left, vectors, factors, own, y_got, y_late, three, x_out, high_ref, low_ref):
    y, core, z, _ = places()
    outer = ring_outer(y)
    bits = [(y >> 2) & 1, (y >> 1) & 1]
    ring_bit = jnp.where(outer, bits[0], bits[1])
    ring_own = jnp.where(outer, own[0, 0, 0], own[0, 0, 1])
    place_rows(high_ref, low_ref, 0, ring_bit, ring_own)
    place_rows(high_ref, low_ref, 0, 1 - ring_bit, jnp.where(y_ahead(y, z), y_got[...], y_late[...]))
    place_rows(high_ref, low_ref, 1, core, own[0, 0, 3])
    place_rows(high_ref, low_ref, 1, 1 - core, three[...])
    x = left[...]
    for panel in (1, 0):
        vector = vectors[panel]
        columns = x.shape[1]
        both = lax.dot_general(
            vector,
            jnp.concatenate(halves(x), axis=1),
            (((0,), (0,)), ((), ())),
            preferred_element_type=f32,
        )
        projected = both[:, :columns] + both[:, columns:]
        scaled = split_times(*halves(factors[panel]), projected)
        x = x - exact_times(vector, scaled)
    x_out[...] = x


def group_kernel(x_in, high_in, low_in, node_y, own, y_pair, x_out, high_ref, low_ref):
    y, core, _, _ = places()
    outer = ring_outer(y)
    bits = [(y >> 2) & 1, (y >> 1) & 1, y & 1, core]
    pair_bit = jnp.where(outer, bits[1], bits[0])
    pair_own = jnp.where(outer, own[0, 0, 1], own[0, 0, 0])
    place_rows(high_ref, low_ref, 0, pair_bit, pair_own)
    place_rows(high_ref, low_ref, 0, 1 - pair_bit, y_pair[1])
    place_rows(high_ref, low_ref, 1, bits[2], own[0, 0, 2])
    place_rows(high_ref, low_ref, 1, 1 - bits[2], y_pair[0])
    x_out[...] = x_in[...]
    terms = [
        (jnp.where(outer, high_in[0], high_ref[0]), jnp.where(outer, low_in[0], low_ref[0])),
        (jnp.where(outer, high_ref[0], high_in[0]), jnp.where(outer, low_ref[0], low_in[0])),
        (high_ref[1], low_ref[1]),
        (high_in[1], low_in[1]),
    ]
    for i, (high, low) in enumerate(terms):
        tree_step(x_out, high, low, node_y.at[0, 0, i], bits[i])


def middle_kernel(x_in, node_y, own, z_got, z_pair, eight, eight_late, x_out, high_out, low_out, high_ref, low_ref):
    y, _, z, x_place = places()
    outer = ring_outer(z)
    row = jnp.where(outer, 0, 1)
    bits = [(z >> 2) & 1, (z >> 1) & 1, z & 1]
    ring_bit = jnp.where(outer, bits[0], bits[1])
    pair_bit = jnp.where(outer, bits[1], bits[0])
    x_out[...] = x_in[...]
    for i in range(3):
        place_rows(high_ref, low_ref, i, bits[i], own[0, 0, 4 + i])
    place_rows(high_ref, low_ref, row, 1 - ring_bit, z_got[...])
    place_rows(high_ref, low_ref, 1 - row, 1 - pair_bit, z_pair[1])
    place_rows(high_ref, low_ref, 2, 1 - bits[2], z_pair[0])
    last = x_place & 1
    place_rows(high_out, low_out, 0, last, own[0, 0, 8])
    place_rows(high_out, low_out, 0, 1 - last, jnp.where(eight_ahead(y, z), eight[...], eight_late[...]))
    for i in range(3):
        tree_step(x_out, high_ref[i], low_ref[i], node_y.at[0, 0, 4 + i], bits[i])


def leaf_kernel(
    x_in, high_in, low_in, node_y, own, seven, leaf_v, leaf_t, leaf_map, out,
    x_ref, high_ref, low_ref, map_ref, sem,
):
    _, _, _, x_place = places()
    load = pltpu.make_async_copy(leaf_map, map_ref, sem)
    load.start()
    bit = (x_place >> 1) & 1
    last = x_place & 1
    x_ref[...] = x_in[...]
    place_rows(high_ref, low_ref, 0, bit, own[0, 0, 7])
    place_rows(high_ref, low_ref, 0, 1 - bit, seven[...])
    tree_step(x_ref, high_ref[0], low_ref[0], node_y.at[0, 0, 7], bit)
    load.wait()
    flipped = map_ref[0, 0] != lax.axis_index("leaf")
    tree_step(x_ref, high_in[0], low_in[0], node_y.at[0, 0, 8], jnp.where(flipped, 1 - last, last))
    x = x_ref[...]
    projected = lax.dot_general(
        leaf_v[:256], x.astype(bf16), (((0,), (0,)), ((), ())), preferred_element_type=f32
    )
    solved = split_times(*halves(leaf_t[0, 0]), projected).astype(bf16)
    out[:256] = (x - mul(leaf_v[:256], solved)).astype(bf16)
    out[256:] = (-mul(leaf_v[256:], solved)).astype(bf16)


def call(kernel, arrays, outs, scratch=()):
    return pl.pallas_call(
        kernel,
        out_shape=tuple(pltpu.VMEM(shape, dtype) for shape, dtype in outs),
        in_specs=[VMEM] * len(arrays),
        out_specs=(VMEM,) * len(outs),
        scratch_shapes=list(scratch),
        compiler_params=SMALL,
    )(*[in_vmem(array) for array in arrays])


def exchange(block, partner, chosen=lambda y, z: True):
    pairs = []
    for g in range(16):
        for j in range(32):
            place = (g >> 1, g & 1, j >> 2, j & 3)
            if chosen(place[0], place[2]):
                y, core, z, x = partner(*place)
                pairs.append((g * 32 + j, (y * 2 + core) * 32 + z * 4 + x))
    return lax.ppermute(block, ("group", "leaf"), pairs)


def body(left_vectors, panel_vectors, panel_factors, node_y, node_t, leaf_v, leaf_t, leaf_map):
    def y_ring(y, core, z, x):
        return ring_partner(y), core, z, x

    def z_ring(y, core, z, x):
        return y, core, ring_partner(z), x

    def y_next(y, core, z, x):
        return y ^ 1, core, z, x

    def z_next(y, core, z, x):
        return y, core, z ^ 1, x

    def x_far(y, core, z, x):
        return y, core, z, x ^ 3

    def x_next(y, core, z, x):
        return y, core, z, x ^ 1

    def other_core(y, core, z, x):
        return y, 1 - core, z, x

    y_send, z_send, seven, eight, three = pieces(pltpu.with_memory_space_constraint(node_t, pltpu.HBM))
    own = node_t
    y_got = [exchange(y_send, y_ring, y_ahead)]
    eight_got = [exchange(eight, x_next, eight_ahead)]
    z_got = exchange(z_send, z_ring)
    y_got.append(exchange(y_send, y_ring, lambda y, z: not y_ahead(y, z)))
    eight_got.append(exchange(eight, x_next, lambda y, z: not eight_ahead(y, z)))
    three_got = exchange(three, other_core)
    y_pair = exchange(join(own, y_got, 2), y_next)
    z_pair = exchange(join(own, [z_got], 6), z_next)
    seven_got = exchange(seven, x_far)
    term = pltpu.VMEM((2, 256, 256), bf16)
    root, high, low = call(
        root_kernel,
        [left_vectors, panel_vectors, panel_factors, own, *y_got, three_got],
        [((256, 128), f32), ((2, 256, 256), bf16), ((2, 256, 256), bf16)],
    )
    (x,) = call(group_kernel, [root, high, low, node_y, own, y_pair], [((256, 128), f32)], (term, term))
    term = pltpu.VMEM((3, 256, 256), bf16)
    x, high, low = call(
        middle_kernel,
        [x, node_y, own, z_got, z_pair, *eight_got],
        [((256, 128), f32), ((1, 256, 256), bf16), ((1, 256, 256), bf16)],
        (term, term),
    )
    term = pltpu.VMEM((1, 256, 256), bf16)
    return pl.pallas_call(
        leaf_kernel,
        out_shape=jax.ShapeDtypeStruct((512, 128), bf16),
        in_specs=[VMEM] * 8 + [ANY],
        out_specs=VMEM,
        scratch_shapes=[pltpu.VMEM((256, 128), f32), term, term, pltpu.SMEM((1, 1), jnp.int32), pltpu.SemaphoreType.DMA],
        name="leaf_kernel",
        compiler_params=SMALL,
    )(*[in_vmem(array) for array in (x, high, low, node_y, own, seven_got, leaf_v, leaf_t)], leaf_map)


def solution(mesh):
    return jax.shard_map(
        body,
        mesh=mesh,
        in_specs=(
            P(),
            P(),
            P(),
            P("group", "leaf", None, None, None),
            P("group", "leaf", None, None, None),
            P(("group", "leaf"), None),
            P("group", "leaf", None, None),
            P("group", "leaf"),
        ),
        out_specs=P(("group", "leaf"), None),
        check_vma=False,
    )
```

```python
import jax
import jax.numpy as jnp
from jax import lax
from jax.experimental import pallas as pl
from jax.experimental.pallas import tpu as pltpu
from jax.sharding import PartitionSpec as P


ANY = pl.BlockSpec(memory_space=pl.ANY)
VMEM = pl.BlockSpec(memory_space=pltpu.VMEM)
SMEM = pl.BlockSpec(memory_space=pltpu.SMEM)
SMALL = pltpu.CompilerParams(vmem_limit_bytes=8 << 20)
f32 = jnp.float32
bf16 = jnp.bfloat16


def halves(value):
    high = value.astype(bf16)
    low = (value - high.astype(f32)).astype(bf16)
    return high, low


def mul(left, right):
    return jnp.dot(left, right, preferred_element_type=f32)


def exact_times(exact, value):
    columns = value.shape[1]
    both = mul(exact, jnp.concatenate(halves(value), axis=1))
    return both[:, :columns] + both[:, columns:]


def split_times(high, low, value):
    columns = value.shape[1]
    value_high, value_low = halves(value)
    both = mul(high, jnp.concatenate([value_high, value_low], axis=1))
    return both[:, :columns] + both[:, columns:] + mul(low, value_high)


def ring_partner(place):
    return (place + 1) % 8 if place % 2 else (place - 1) % 8


def ring_outer(place):
    return (place & 1) == ((place >> 1) & 1)


def places():
    group = lax.axis_index("group")
    leaf = lax.axis_index("leaf")
    return group >> 1, group & 1, leaf >> 2, leaf & 3


def y_ahead(y, z):
    return (z == 0) | (z == 3)


def eight_ahead(y, z):
    return z == 0


def pieces_kernel(node_t, y_send, z_send, seven, eight, sems):
    y, core, z, _ = places()
    y_level = jnp.where(ring_outer(y), 0, 1)
    z_level = jnp.where(ring_outer(z), 4, 5)
    y_rows = pl.ds(pl.multiple_of(core * 64, 64), 64)
    copies = [
        pltpu.make_async_copy(source, out, sems.at[i])
        for i, (source, out) in enumerate(
            [
                (node_t.at[0, 0, y_level, y_rows], y_send),
                (node_t.at[0, 0, z_level], z_send),
                (node_t.at[0, 0, 7], seven),
                (node_t.at[0, 0, 8], eight),
            ]
        )
    ]
    for copy in copies:
        copy.start()
    for copy in copies:
        copy.wait()


def in_hbm(array):
    return pltpu.with_memory_space_constraint(array, pltpu.HBM)


def in_vmem(array):
    return pltpu.with_memory_space_constraint(array, pltpu.VMEM)


def pieces(node_t):
    shape = pltpu.VMEM((128, 256), f32)
    return pl.pallas_call(
        pieces_kernel,
        out_shape=(pltpu.VMEM((64, 256), f32),) + (shape,) * 3,
        in_specs=[ANY],
        out_specs=(VMEM,) * 4,
        scratch_shapes=[pltpu.SemaphoreType.DMA((4,))],
        name="pieces",
        compiler_params=SMALL,
    )(node_t)


def join_y_kernel(own, got, late, out):
    y, core, z, _ = places()
    out[0] = own[0, 0, 2, pl.ds(pl.multiple_of(core * 64, 64), 64)]
    out[1] = jnp.where(y_ahead(y, z), got[...], late[...])


def join_z_kernel(own, got, out):
    out[0] = own[0, 0, 6]
    out[1] = got[...]


def join_core_kernel(own, y_joined, y_pair, out):
    out[:128] = own[0, 0, 3]
    out[128:192] = y_joined[1]
    out[192:256] = y_pair[0]
    out[256:] = y_pair[1]


def place_rows(high_ref, low_ref, slot, bit, value, inner=0):
    rows = pl.ds(pl.multiple_of(bit * 128 + inner, 64), value.shape[0])
    high, low = halves(value)
    high_ref[slot, rows] = high
    low_ref[slot, rows] = low


def tree_step(x_ref, high, low, reflect, lower):
    weighted = split_times(high, low, x_ref[...])

    @pl.when(lower == 1)
    def _():
        x_ref[...] = -exact_times(reflect[...], weighted)

    @pl.when(lower == 0)
    def _():
        x_ref[...] = x_ref[...] - weighted


def back_panels(left, vectors, factors, x_out):
    x = left[...]
    for panel in (1, 0):
        vector = vectors[panel]
        columns = x.shape[1]
        both = lax.dot_general(
            vector,
            jnp.concatenate(halves(x), axis=1),
            (((0,), (0,)), ((), ())),
            preferred_element_type=f32,
        )
        projected = both[:, :columns] + both[:, columns:]
        scaled = split_times(*halves(factors[panel]), projected)
        x = x - exact_times(vector, scaled)
    x_out[...] = x


def early_root_kernel(left, vectors, factors, x_out, left_ref, vectors_ref, factors_ref, sems):
    _, core, _, _ = places()

    @pl.when(core == 1)
    def _():
        copies = [
            pltpu.make_async_copy(source, target, sems.at[i])
            for i, (source, target) in enumerate(
                [(left, left_ref), (vectors, vectors_ref), (factors, factors_ref)]
            )
        ]
        for copy in copies:
            copy.start()
        for copy in copies:
            copy.wait()
        back_panels(left_ref, vectors_ref, factors_ref, x_out)


def root_kernel(left, vectors, factors, x_out):
    _, core, _, _ = places()

    @pl.when(core == 0)
    def _():
        back_panels(left, vectors, factors, x_out)


def group_kernel(x_early, x_in, node_y, own, y_joined, y_pair, core_got, x_out, high_ref, low_ref):
    y, core, _, _ = places()
    outer = ring_outer(y)
    row = jnp.where(outer, 0, 1)
    bits = [(y >> 2) & 1, (y >> 1) & 1, y & 1, core]
    ring_bit = jnp.where(outer, bits[0], bits[1])
    pair_bit = jnp.where(outer, bits[1], bits[0])
    for i in range(4):
        place_rows(high_ref, low_ref, i, bits[i], own[0, 0, i])
    for slot, bit, mine, theirs in (
        (row, ring_bit, y_joined[1], core_got[128:192]),
        (2, bits[2], y_pair[0], core_got[192:256]),
        (1 - row, pair_bit, y_pair[1], core_got[256:]),
    ):
        place_rows(high_ref, low_ref, slot, 1 - bit, mine, core * 64)
        place_rows(high_ref, low_ref, slot, 1 - bit, theirs, 64 - core * 64)
    place_rows(high_ref, low_ref, 3, 1 - core, core_got[:128])
    x_out[...] = jnp.where(core == 1, x_early[...], x_in[...])
    for i in range(4):
        tree_step(x_out, high_ref[i], low_ref[i], node_y.at[0, 0, i], bits[i])


def middle_kernel(
    x_in, node_y, own, z_got, z_pair, eight, eight_late, leaf_v, leaf_t,
    x_out, high_out, low_out, own_high, own_low, turned, high_ref, low_ref,
):
    y, _, z, x_place = places()
    outer = ring_outer(z)
    row = jnp.where(outer, 0, 1)
    bits = [(z >> 2) & 1, (z >> 1) & 1, z & 1]
    ring_bit = jnp.where(outer, bits[0], bits[1])
    pair_bit = jnp.where(outer, bits[1], bits[0])
    x_out[...] = x_in[...]
    for i in range(3):
        place_rows(high_ref, low_ref, i, bits[i], own[0, 0, 4 + i])
    place_rows(high_ref, low_ref, row, 1 - ring_bit, z_got[...])
    place_rows(high_ref, low_ref, 1 - row, 1 - pair_bit, z_pair[1])
    place_rows(high_ref, low_ref, 2, 1 - bits[2], z_pair[0])
    last = x_place & 1
    place_rows(high_out, low_out, 0, last, own[0, 0, 8])
    place_rows(high_out, low_out, 0, 1 - last, jnp.where(eight_ahead(y, z), eight[...], eight_late[...]))
    for i in range(3):
        tree_step(x_out, high_ref[i], low_ref[i], node_y.at[0, 0, 4 + i], bits[i])
    high_out[1], low_out[1] = halves(leaf_t[0, 0])
    own_high[...], own_low[...] = halves(own[0, 0, 7])
    turned[...] = leaf_v[:256].T


def leaf_kernel(
    x_in, high_in, low_in, own_high, own_low, turned, node_y, seven, leaf_v, leaf_map, out,
    x_ref, out_ref, sems,
):
    _, _, _, x_place = places()
    bit = (x_place >> 1) & 1
    last = x_place & 1
    x_ref[...] = x_in[...]
    high, low = [
        jnp.where(bit == 0, jnp.concatenate([mine, other]), jnp.concatenate([other, mine]))
        for mine, other in zip((own_high[...], own_low[...]), halves(seven[...]))
    ]
    tree_step(x_ref, high, low, node_y.at[0, 0, 7], bit)
    flipped = leaf_map[0, 0] != lax.axis_index("leaf")
    tree_step(x_ref, high_in[0], low_in[0], node_y.at[0, 0, 8], jnp.where(flipped, 1 - last, last))
    x = x_ref[...]
    projected = mul(turned[...], x.astype(bf16))
    solved = split_times(high_in[1], low_in[1], projected).astype(bf16)
    out_ref[256:] = (-mul(leaf_v[256:], solved)).astype(bf16)
    store_low = pltpu.make_async_copy(out_ref.at[pl.ds(256, 256)], out.at[pl.ds(256, 256)], sems.at[0])
    store_low.start()
    out_ref[:256] = (x - mul(leaf_v[:256], solved)).astype(bf16)
    store_top = pltpu.make_async_copy(out_ref.at[pl.ds(0, 256)], out.at[pl.ds(0, 256)], sems.at[1])
    store_top.start()
    store_low.wait()
    store_top.wait()


def call(kernel, arrays, outs, scratch=()):
    return pl.pallas_call(
        kernel,
        out_shape=tuple(pltpu.VMEM(shape, dtype) for shape, dtype in outs),
        in_specs=[VMEM] * len(arrays),
        out_specs=(VMEM,) * len(outs),
        scratch_shapes=list(scratch),
        compiler_params=SMALL,
    )(*[in_vmem(array) for array in arrays])


def exchange(block, partner, chosen=lambda y, z: True):
    pairs = []
    for g in range(16):
        for j in range(32):
            place = (g >> 1, g & 1, j >> 2, j & 3)
            if chosen(place[0], place[2]):
                y, core, z, x = partner(*place)
                pairs.append((g * 32 + j, (y * 2 + core) * 32 + z * 4 + x))
    return lax.ppermute(block, ("group", "leaf"), pairs)


def body(left_vectors, panel_vectors, panel_factors, node_y, node_t, leaf_v, leaf_t, leaf_map):
    def y_ring(y, core, z, x):
        return ring_partner(y), core, z, x

    def z_ring(y, core, z, x):
        return y, core, ring_partner(z), x

    def y_next(y, core, z, x):
        return y ^ 1, core, z, x

    def z_next(y, core, z, x):
        return y, core, z ^ 1, x

    def x_far(y, core, z, x):
        return y, core, z, x ^ 3

    def x_next(y, core, z, x):
        return y, core, z, x ^ 1

    def other_core(y, core, z, x):
        return y, 1 - core, z, x

    y_send, z_send, seven, eight = pieces(pltpu.with_memory_space_constraint(node_t, pltpu.HBM))
    own = node_t
    y_got = [exchange(y_send, y_ring, y_ahead)]
    eight_got = [exchange(eight, x_next, eight_ahead)]
    z_got = exchange(z_send, z_ring)
    y_got.append(exchange(y_send, y_ring, lambda y, z: not y_ahead(y, z)))
    eight_got.append(exchange(eight, x_next, lambda y, z: not eight_ahead(y, z)))
    (y_joined,) = call(join_y_kernel, [own, *y_got], [((2, 64, 256), f32)])
    y_pair = exchange(y_joined, y_next)
    (z_joined,) = call(join_z_kernel, [own, z_got], [((2, 128, 256), f32)])
    z_pair = exchange(z_joined, z_next)
    seven_got = exchange(seven, x_far)
    early_root = pl.pallas_call(
        early_root_kernel,
        out_shape=pltpu.VMEM((256, 128), f32),
        in_specs=[ANY] * 3,
        out_specs=VMEM,
        scratch_shapes=[
            pltpu.VMEM((256, 128), f32),
            pltpu.VMEM((2, 256, 128), bf16),
            pltpu.VMEM((2, 128, 128), f32),
            pltpu.SemaphoreType.DMA((3,)),
        ],
        name="early_root_kernel",
        compiler_params=SMALL,
    )(*[in_hbm(array) for array in (left_vectors, panel_vectors, panel_factors)])
    (core_joined,) = call(join_core_kernel, [own, y_joined, y_pair], [((320, 256), f32)])
    core_got = exchange(core_joined, other_core)
    (root,) = call(root_kernel, [left_vectors, panel_vectors, panel_factors], [((256, 128), f32)])
    term = pltpu.VMEM((4, 256, 256), bf16)
    (x,) = call(
        group_kernel,
        [early_root, root, node_y, own, y_joined, y_pair, core_got],
        [((256, 128), f32)],
        (term, term),
    )
    term = pltpu.VMEM((3, 256, 256), bf16)
    half = ((128, 256), bf16)
    pair = ((2, 256, 256), bf16)
    x, *factors = call(
        middle_kernel,
        [x, node_y, own, z_got, z_pair, *eight_got, leaf_v, leaf_t],
        [((256, 128), f32), pair, pair, half, half, ((256, 256), bf16)],
        (term, term),
    )
    return pl.pallas_call(
        leaf_kernel,
        out_shape=jax.ShapeDtypeStruct((512, 128), bf16),
        in_specs=[VMEM] * 9 + [SMEM],
        out_specs=ANY,
        scratch_shapes=[
            pltpu.VMEM((256, 128), f32),
            pltpu.VMEM((512, 128), bf16),
            pltpu.SemaphoreType.DMA((2,)),
        ],
        name="leaf_kernel",
        compiler_params=SMALL,
    )(*[in_vmem(array) for array in (x, *factors, node_y, seven_got, leaf_v)], leaf_map)


def solution(mesh):
    return jax.shard_map(
        body,
        mesh=mesh,
        in_specs=(
            P(),
            P(),
            P(),
            P("group", "leaf", None, None, None),
            P("group", "leaf", None, None, None),
            P(("group", "leaf"), None),
            P("group", "leaf", None, None),
            P("group", "leaf"),
        ),
        out_specs=P(("group", "leaf"), None),
        check_vma=False,
    )
```

```python
import jax
import jax.numpy as jnp
from jax import lax
from jax.experimental import pallas as pl
from jax.experimental.pallas import tpu as pltpu
from jax.sharding import PartitionSpec as P


ANY = pl.BlockSpec(memory_space=pl.ANY)
VMEM = pl.BlockSpec(memory_space=pltpu.VMEM)
SMEM = pl.BlockSpec(memory_space=pltpu.SMEM)
SMALL = pltpu.CompilerParams(vmem_limit_bytes=8 << 20)
f32 = jnp.float32
bf16 = jnp.bfloat16


def halves(value):
    high = value.astype(bf16)
    low = (value - high.astype(f32)).astype(bf16)
    return high, low


def mul(left, right):
    return jnp.dot(left, right, preferred_element_type=f32)


def exact_times(exact, value):
    columns = value.shape[1]
    both = mul(exact, jnp.concatenate(halves(value), axis=1))
    return both[:, :columns] + both[:, columns:]


def split_times(high, low, value):
    columns = value.shape[1]
    value_high, value_low = halves(value)
    both = mul(high, jnp.concatenate([value_high, value_low], axis=1))
    return both[:, :columns] + both[:, columns:] + mul(low, value_high)


def ring_partner(place):
    return (place + 1) % 8 if place % 2 else (place - 1) % 8


def ring_outer(place):
    return (place & 1) == ((place >> 1) & 1)


def places():
    group = lax.axis_index("group")
    leaf = lax.axis_index("leaf")
    return group >> 1, group & 1, leaf >> 2, leaf & 3


def y_ahead(y, z):
    return z == 0


def eight_ahead(y, z):
    return (z == 0) | (z == 3)


def pieces_kernel(node_t, y_send, z_send, seven, eight, three, sems):
    y, _, z, _ = places()
    y_level = jnp.where(ring_outer(y), 0, 1)
    z_level = jnp.where(ring_outer(z), 4, 5)
    copies = [
        pltpu.make_async_copy(node_t.at[0, 0, level], out, sems.at[i])
        for i, (level, out) in enumerate(
            [(y_level, y_send), (z_level, z_send), (7, seven), (8, eight), (3, three)]
        )
    ]
    for copy in copies:
        copy.start()
    for copy in copies:
        copy.wait()


def in_vmem(array):
    return pltpu.with_memory_space_constraint(array, pltpu.VMEM)


def pieces(node_t):
    shape = pltpu.VMEM((128, 256), f32)
    return pl.pallas_call(
        pieces_kernel,
        out_shape=(shape,) * 5,
        in_specs=[ANY],
        out_specs=(VMEM,) * 5,
        scratch_shapes=[pltpu.SemaphoreType.DMA((5,))],
        name="pieces",
        compiler_params=SMALL,
    )(node_t)


def join(own, received, level):
    def kernel(own, *refs):
        out = refs[-1]
        out[0] = own[0, 0, level]
        if len(refs) == 2:
            out[1] = refs[0][...]
        else:
            y, _, z, _ = places()
            out[1] = jnp.where(y_ahead(y, z), refs[0][...], refs[1][...])

    return pl.pallas_call(
        kernel,
        out_shape=pltpu.VMEM((2, 128, 256), f32),
        in_specs=[VMEM] * (1 + len(received)),
        out_specs=VMEM,
        compiler_params=SMALL,
    )(*[in_vmem(array) for array in (own, *received)])


def place_rows(high_ref, low_ref, slot, bit, value):
    rows = pl.ds(pl.multiple_of(bit * 128, 128), 128)
    high, low = halves(value)
    high_ref[slot, rows] = high
    low_ref[slot, rows] = low


def tree_step(x_ref, high, low, reflect, lower):
    weighted = split_times(high, low, x_ref[...])

    @pl.when(lower == 1)
    def _():
        x_ref[...] = -exact_times(reflect[...], weighted)

    @pl.when(lower == 0)
    def _():
        x_ref[...] = x_ref[...] - weighted


def root_kernel(left, vectors, factors, own, y_got, y_late, three, x_out, high_ref, low_ref):
    y, core, z, _ = places()
    outer = ring_outer(y)
    bits = [(y >> 2) & 1, (y >> 1) & 1]
    ring_bit = jnp.where(outer, bits[0], bits[1])
    ring_own = jnp.where(outer, own[0, 0, 0], own[0, 0, 1])
    place_rows(high_ref, low_ref, 0, ring_bit, ring_own)
    place_rows(high_ref, low_ref, 0, 1 - ring_bit, jnp.where(y_ahead(y, z), y_got[...], y_late[...]))
    place_rows(high_ref, low_ref, 1, core, own[0, 0, 3])
    place_rows(high_ref, low_ref, 1, 1 - core, three[...])
    x = left[...]
    for panel in (1, 0):
        vector = vectors[panel]
        columns = x.shape[1]
        both = lax.dot_general(
            vector,
            jnp.concatenate(halves(x), axis=1),
            (((0,), (0,)), ((), ())),
            preferred_element_type=f32,
        )
        projected = both[:, :columns] + both[:, columns:]
        scaled = split_times(*halves(factors[panel]), projected)
        x = x - exact_times(vector, scaled)
    x_out[...] = x


def group_kernel(x_in, high_in, low_in, node_y, own, y_pair, x_out, high_ref, low_ref):
    y, core, _, _ = places()
    outer = ring_outer(y)
    bits = [(y >> 2) & 1, (y >> 1) & 1, y & 1, core]
    pair_bit = jnp.where(outer, bits[1], bits[0])
    pair_own = jnp.where(outer, own[0, 0, 1], own[0, 0, 0])
    place_rows(high_ref, low_ref, 0, pair_bit, pair_own)
    place_rows(high_ref, low_ref, 0, 1 - pair_bit, y_pair[1])
    place_rows(high_ref, low_ref, 1, bits[2], own[0, 0, 2])
    place_rows(high_ref, low_ref, 1, 1 - bits[2], y_pair[0])
    x_out[...] = x_in[...]
    terms = [
        (jnp.where(outer, high_in[0], high_ref[0]), jnp.where(outer, low_in[0], low_ref[0])),
        (jnp.where(outer, high_ref[0], high_in[0]), jnp.where(outer, low_ref[0], low_in[0])),
        (high_ref[1], low_ref[1]),
        (high_in[1], low_in[1]),
    ]
    for i, (high, low) in enumerate(terms):
        tree_step(x_out, high, low, node_y.at[0, 0, i], bits[i])


def middle_kernel(
    x_in, node_y, own, z_got, z_pair, eight, eight_late, leaf_v, leaf_t,
    x_out, high_out, low_out, own_high, own_low, turned, high_ref, low_ref,
):
    y, _, z, x_place = places()
    outer = ring_outer(z)
    row = jnp.where(outer, 0, 1)
    bits = [(z >> 2) & 1, (z >> 1) & 1, z & 1]
    ring_bit = jnp.where(outer, bits[0], bits[1])
    pair_bit = jnp.where(outer, bits[1], bits[0])
    x_out[...] = x_in[...]
    for i in range(3):
        place_rows(high_ref, low_ref, i, bits[i], own[0, 0, 4 + i])
    place_rows(high_ref, low_ref, row, 1 - ring_bit, z_got[...])
    place_rows(high_ref, low_ref, 1 - row, 1 - pair_bit, z_pair[1])
    place_rows(high_ref, low_ref, 2, 1 - bits[2], z_pair[0])
    last = x_place & 1
    place_rows(high_out, low_out, 0, last, own[0, 0, 8])
    place_rows(high_out, low_out, 0, 1 - last, jnp.where(eight_ahead(y, z), eight[...], eight_late[...]))
    for i in range(3):
        tree_step(x_out, high_ref[i], low_ref[i], node_y.at[0, 0, 4 + i], bits[i])
    high_out[1], low_out[1] = halves(leaf_t[0, 0])
    own_high[...], own_low[...] = halves(own[0, 0, 7])
    turned[...] = leaf_v[:256].T


def leaf_kernel(
    x_in, high_in, low_in, own_high, own_low, turned, node_y, seven, leaf_v, leaf_map, out,
    x_ref, out_ref, sems,
):
    _, _, _, x_place = places()
    bit = (x_place >> 1) & 1
    last = x_place & 1
    x_ref[...] = x_in[...]
    high, low = [
        jnp.where(bit == 0, jnp.concatenate([mine, other]), jnp.concatenate([other, mine]))
        for mine, other in zip((own_high[...], own_low[...]), halves(seven[...]))
    ]
    tree_step(x_ref, high, low, node_y.at[0, 0, 7], bit)
    flipped = leaf_map[0, 0] != lax.axis_index("leaf")
    tree_step(x_ref, high_in[0], low_in[0], node_y.at[0, 0, 8], jnp.where(flipped, 1 - last, last))
    x = x_ref[...]
    projected = mul(turned[...], x.astype(bf16))
    solved = split_times(high_in[1], low_in[1], projected).astype(bf16)
    out_ref[256:] = (-mul(leaf_v[256:], solved)).astype(bf16)
    store_low = pltpu.make_async_copy(out_ref.at[pl.ds(256, 256)], out.at[pl.ds(256, 256)], sems.at[0])
    store_low.start()
    out_ref[:256] = (x - mul(leaf_v[:256], solved)).astype(bf16)
    store_top = pltpu.make_async_copy(out_ref.at[pl.ds(0, 256)], out.at[pl.ds(0, 256)], sems.at[1])
    store_top.start()
    store_low.wait()
    store_top.wait()


def call(kernel, arrays, outs, scratch=()):
    return pl.pallas_call(
        kernel,
        out_shape=tuple(pltpu.VMEM(shape, dtype) for shape, dtype in outs),
        in_specs=[VMEM] * len(arrays),
        out_specs=(VMEM,) * len(outs),
        scratch_shapes=list(scratch),
        compiler_params=SMALL,
    )(*[in_vmem(array) for array in arrays])


def exchange(block, partner, chosen=lambda y, z: True):
    pairs = []
    for g in range(16):
        for j in range(32):
            place = (g >> 1, g & 1, j >> 2, j & 3)
            if chosen(place[0], place[2]):
                y, core, z, x = partner(*place)
                pairs.append((g * 32 + j, (y * 2 + core) * 32 + z * 4 + x))
    return lax.ppermute(block, ("group", "leaf"), pairs)


def body(left_vectors, panel_vectors, panel_factors, node_y, node_t, leaf_v, leaf_t, leaf_map):
    def y_ring(y, core, z, x):
        return ring_partner(y), core, z, x

    def z_ring(y, core, z, x):
        return y, core, ring_partner(z), x

    def y_next(y, core, z, x):
        return y ^ 1, core, z, x

    def z_next(y, core, z, x):
        return y, core, z ^ 1, x

    def x_far(y, core, z, x):
        return y, core, z, x ^ 3

    def x_next(y, core, z, x):
        return y, core, z, x ^ 1

    def other_core(y, core, z, x):
        return y, 1 - core, z, x

    y_send, z_send, seven, eight, three = pieces(pltpu.with_memory_space_constraint(node_t, pltpu.HBM))
    own = node_t
    y_got = [exchange(y_send, y_ring, y_ahead)]
    eight_got = [exchange(eight, x_next, eight_ahead)]
    z_got = exchange(z_send, z_ring)
    y_got.append(exchange(y_send, y_ring, lambda y, z: not y_ahead(y, z)))
    eight_got.append(exchange(eight, x_next, lambda y, z: not eight_ahead(y, z)))
    three_got = exchange(three, other_core)
    y_pair = exchange(join(own, y_got, 2), y_next)
    z_pair = exchange(join(own, [z_got], 6), z_next)
    seven_got = exchange(seven, x_far)
    term = pltpu.VMEM((2, 256, 256), bf16)
    root, high, low = call(
        root_kernel,
        [left_vectors, panel_vectors, panel_factors, own, *y_got, three_got],
        [((256, 128), f32), ((2, 256, 256), bf16), ((2, 256, 256), bf16)],
    )
    (x,) = call(group_kernel, [root, high, low, node_y, own, y_pair], [((256, 128), f32)], (term, term))
    term = pltpu.VMEM((3, 256, 256), bf16)
    half = ((128, 256), bf16)
    pair = ((2, 256, 256), bf16)
    x, *factors = call(
        middle_kernel,
        [x, node_y, own, z_got, z_pair, *eight_got, leaf_v, leaf_t],
        [((256, 128), f32), pair, pair, half, half, ((256, 256), bf16)],
        (term, term),
    )
    return pl.pallas_call(
        leaf_kernel,
        out_shape=jax.ShapeDtypeStruct((512, 128), bf16),
        in_specs=[VMEM] * 9 + [SMEM],
        out_specs=ANY,
        scratch_shapes=[
            pltpu.VMEM((256, 128), f32),
            pltpu.VMEM((512, 128), bf16),
            pltpu.SemaphoreType.DMA((2,)),
        ],
        name="leaf_kernel",
        compiler_params=SMALL,
    )(*[in_vmem(array) for array in (x, *factors, node_y, seven_got, leaf_v)], leaf_map)


def solution(mesh):
    return jax.shard_map(
        body,
        mesh=mesh,
        in_specs=(
            P(),
            P(),
            P(),
            P("group", "leaf", None, None, None),
            P("group", "leaf", None, None, None),
            P(("group", "leaf"), None),
            P("group", "leaf", None, None),
            P("group", "leaf"),
        ),
        out_specs=P(("group", "leaf"), None),
        check_vma=False,
    )
```
